256 devices in a mesh: sub: 64 (over y_lo, z, x), blk: 4 (over y_hi, core).
Axes of the slice: x: 4, y: 4 (y_hi: 2, y_lo: 2; y = y_hi * 2 + y_lo), z: 8, core: 2. Of those that a mesh axis runs over, the one named last changes fastest.
Arguments:
- residual: float32 [32, 131072], P(None, ('sub', 'blk')), may hold values from -6 to 6
- fine_inverse: float32 [64, 2560, 2048], P('sub', None, 'blk'), may hold values from -1 to 1.1
- coarse_inverse: float32 [16384, 4, 4096], P('sub', 'blk'), may hold values from -0.5 to 0.5, as said below
- wanted_rows: int32 [64, 2, 256], P('sub'), may hold values from 0 to 2047
- wanted_count: int32 [64, 2], P('sub'), may hold values from 32 to 256, as said below
- aggregate: int32 [131072], P(('sub', 'blk')), may hold values from 0 to 255
Outputs:
- preconditioned: float32 [32, 131072], P(None, ('sub', 'blk'))
The draws below stay inside these ranges and needn't reach their ends.
Inputs may be any that keep to these rules, and one draw needn't show every extreme that they name: M of the steps is symmetric: coarse_inverse[i, b, s * 64 + q] equals coarse_inverse[s * 256 + b * 64 + q, b2, s2 * 64 + q2] where i = s2 * 256 + b2 * 64 + q2. `wanted_count`: counts vary from side to side; in every draw some subdomain other than the first and last takes exactly 256 rows from one side.
All inputs are finite; a program needn't handle non-finite values.
Results may differ from the reference program's by a relative error of at most 0.000052.
Values sent between devices are 32-bit elements; how exact they have to be, the bound alone decides.
A program may use at most 64 MiB of HBM per device.

```python
import math
import jax
import jax.numpy as jnp
from jax import lax

PROBES = 32
OWN = 2048
HMAX = 256
CPS = 256
SUBDOMAINS = 64
EXT = 2560
ROWS = 131072
NC = 16384
CPART = 64
N_BLK = 4


def draw_fine_inverse(key, part):
    noise_field = jnp.clip(jax.random.normal(key, (SUBDOMAINS, EXT, OWN), jnp.float32), -5.0, 5.0)
    row_ids = lax.broadcasted_iota(jnp.int32, (1, EXT, OWN), 1)
    col_ids = lax.broadcasted_iota(jnp.int32, (1, EXT, OWN), 2)
    diagonal = (row_ids == col_ids + HMAX).astype(jnp.float32)
    return 0.6 * diagonal + noise_field * (0.6 / math.sqrt(EXT))


def draw_coarse_inverse(key, part):
    noise_field = jnp.clip(jax.random.normal(key, (NC, NC), jnp.float32), -5.0, 5.0)
    mirrored = noise_field + noise_field.T
    row_ids = lax.broadcasted_iota(jnp.int32, (NC, NC), 0)
    col_ids = lax.broadcasted_iota(jnp.int32, (NC, NC), 1)
    symmetric = 0.3 * (row_ids == col_ids).astype(jnp.float32) + mirrored * (0.3 / math.sqrt(2.0 * NC))
    groups = CPS // CPART
    grouped = symmetric.reshape(NC, SUBDOMAINS, groups, CPART).transpose(0, 2, 1, 3)
    return grouped.reshape(NC, groups, SUBDOMAINS * CPART)


def draw_wanted_count(key, part):
    key_counts, key_sub, key_side = jax.random.split(key, 3)
    counts = jax.random.randint(key_counts, (SUBDOMAINS, 2), HMAX // 8, HMAX + 1, dtype=jnp.int32)
    chosen_sub = jax.random.randint(key_sub, (), 1, SUBDOMAINS - 1, dtype=jnp.int32)
    chosen_side = jax.random.randint(key_side, (), 0, 2, dtype=jnp.int32)
    sub_ids = lax.broadcasted_iota(jnp.int32, (SUBDOMAINS, 2), 0)
    side_ids = lax.broadcasted_iota(jnp.int32, (SUBDOMAINS, 2), 1)
    return jnp.where((sub_ids == chosen_sub) & (side_ids == chosen_side), HMAX, counts)


def touch_ends(values, stream_key, least, top_value):
    extent = values.shape
    place = [jax.random.randint(jax.random.fold_in(stream_key, axis), (), 0, extent[axis]) for axis in range(len(extent))]
    values = values.at[tuple(place)].set(least)
    longest = extent.index(max(extent))
    place[longest] = (place[longest] + 1) % extent[longest]
    return values.at[tuple(place)].set(top_value)


def level_of(stream_key, shape, pieces, low, top_value):
    level = 1.0
    for axis_at, shards_of in pieces:
        draws = jax.random.uniform(jax.random.fold_in(jax.random.fold_in(stream_key, 6), axis_at), (shards_of,), jnp.float32, low / len(pieces), top_value / len(pieces))
        level = level * jnp.repeat(jnp.exp(draws), shape[axis_at] // shards_of).reshape((-1,) + (1,) * (len(shape) - 1 - axis_at))
    return level


def noise(rng, dims, spread, bound, pieces=(), kind=jnp.bfloat16):
    level = level_of(rng, dims, pieces, -0.22, 0.18) if pieces else 1.0
    drawn = jax.random.normal(rng, dims, jnp.float32) * spread * level
    return jnp.minimum(jnp.maximum(drawn, -bound), bound).astype(kind)


def setup_inputs(seed: int = 0) -> dict:
    arg_keys = jax.random.split(jax.random.key(seed), 7)
    residual = noise(arg_keys[0], (PROBES, ROWS), 1.0, 6.0, ((1, 256),), jnp.float32)
    fine_inverse = draw_fine_inverse(jax.random.fold_in(arg_keys[6], 71), 0)
    coarse_inverse = draw_coarse_inverse(jax.random.fold_in(arg_keys[6], 71), 0)
    wanted_rows = touch_ends(jax.random.randint(arg_keys[3], (SUBDOMAINS, 2, HMAX), 0, OWN), jax.random.fold_in(arg_keys[3], 1), 0, OWN - 1).astype(jnp.int32)
    wanted_count = draw_wanted_count(jax.random.fold_in(arg_keys[6], 71), 0)
    aggregate = touch_ends(jax.random.randint(arg_keys[5], (ROWS,), 0, CPS), jax.random.fold_in(arg_keys[5], 1), 0, CPS - 1).astype(jnp.int32)
    return {"residual": residual, "fine_inverse": fine_inverse, "coarse_inverse": coarse_inverse, "wanted_rows": wanted_rows, "wanted_count": wanted_count, "aggregate": aggregate}


def pick_rows(source, row_lists, row_totals):
    picked = jnp.take_along_axis(source, row_lists[None, :, :], axis=2)
    slot_ids = jnp.arange(HMAX, dtype=jnp.int32)
    kept_mask = slot_ids[None, :] < row_totals[:, None]
    return jnp.where(kept_mask[None, :, :], picked, jnp.zeros_like(picked))


def reference(residual, fine_inverse, coarse_inverse, wanted_rows, wanted_count, aggregate):
    probes = residual.shape[0]
    blocks = residual.reshape(probes, SUBDOMAINS, OWN)
    zeros_block = jnp.zeros((probes, 1, OWN), jnp.float32)
    left_blocks = jnp.concatenate([zeros_block, blocks[:, :-1, :]], axis=1)
    right_blocks = jnp.concatenate([blocks[:, 1:, :], zeros_block], axis=1)
    left_halo = pick_rows(left_blocks, wanted_rows[:, 0, :], wanted_count[:, 0])
    right_halo = pick_rows(right_blocks, wanted_rows[:, 1, :], wanted_count[:, 1])
    extended = jnp.concatenate([left_halo, blocks, right_halo], axis=2)
    fine_part = jnp.einsum("pse,seo->pso", extended, fine_inverse, precision=lax.Precision.HIGHEST)
    dof_ids = (jnp.arange(ROWS, dtype=jnp.int32) // OWN) * CPS + aggregate
    coarse_rhs = jax.ops.segment_sum(residual.T, dof_ids, num_segments=NC)
    ordered = coarse_rhs.reshape(SUBDOMAINS, N_BLK, CPART, probes).transpose(1, 0, 2, 3).reshape(NC, probes)
    flat_inverse = coarse_inverse.reshape(NC, NC)
    coarse_solution = jnp.dot(flat_inverse, ordered, precision=lax.Precision.HIGHEST, preferred_element_type=jnp.float32)
    lifted = coarse_solution[dof_ids, :]
    return fine_part.reshape(probes, ROWS) + lifted.T
```

```python
import jax
import jax.numpy as jnp
from jax import lax
from jax.experimental import pallas as pl
from jax.experimental.pallas import tpu as pltpu
from jax.sharding import PartitionSpec as P

NX, NZ, NY = 4, 8, 2
NB = 4
NSUB = NX * NZ * NY
PR = 32
BL = 512
CS = 256
HM = 256
F32, BF16 = jnp.float32, jnp.bfloat16
MESH = pl.DeviceIdType.MESH
Z_ORDER = (0, 1, 7, 2, 6, 3, 5, 4)
NN = (((1,), (0,)), ((), ()))
NT = (((1,), (1,)), ((), ()))


def mm(a, b, dims=NN):
    return lax.dot_general(a, b, dims, preferred_element_type=F32)


def split2(v):
    hi = v.astype(BF16)
    return hi, (v - hi.astype(F32)).astype(BF16)


def split3(v):
    hi = v.astype(BF16)
    rest = v - hi.astype(F32)
    mid = rest.astype(BF16)
    return hi, mid, (rest - mid.astype(F32)).astype(BF16)


def exact(v, onehot, dims=NN):
    n = v.shape[0]
    r = mm(jnp.concatenate(split3(v), axis=0), onehot, dims)
    return (r[:n] + r[n : 2 * n]) + r[2 * n :]


def three(v, w, dims=NN):
    n = v.shape[0]
    vh, vl = split2(v)
    wh, wl = split2(w)
    r = mm(jnp.concatenate([vh, vl], axis=0), wh, dims)
    return (r[:n] + r[n:]) + mm(vh, wl, dims)


def kernel(
    res_ref, agg_ref, want_ref, count_ref, m_hbm, f_hbm, out_ref,
    mbuf, fown, fmar, own, qout, ybuf, xg, nwant, hout, hin, ysum,
    m_sem, f_sem, g_sem, own_s, own_r, y_s, y_r, z_s, z_r, x_s, x_r, w_s, w_r, h_s, h_r, a_s, a_r,
):
    s = lax.axis_index("sub")
    b = lax.axis_index("blk")
    yl = s // (NZ * NX)
    z = lax.rem(s // NX, NZ)
    x = lax.rem(s, NX)
    mate = lax.rem(s + NZ * NX, NSUB)

    def zpos(d):
        return lax.rem(z + d, NZ)

    def at_z(d):
        return yl * (NZ * NX) + zpos(d) * NX + x

    def at_x(d):
        return s - x + lax.rem(x + d, NX)

    def at_b(d):
        return lax.rem(b + d, NB)

    nxt, prv = lax.rem(s + 1, NSUB), lax.rem(s + NSUB - 1, NSUB)

    partners = [(s, at_b(i)) for i in range(1, NB)] + [(mate, at_b(i)) for i in range(NB)]
    partners += [(at_z(d), b) for d in range(1, NZ)] + [(at_x(d), b) for d in range(1, NX)]
    partners += [(nxt, b), (prv, b)]
    barrier = pltpu.get_barrier_semaphore()
    for p in partners:
        pl.semaphore_signal(barrier, inc=1, device_id=p, device_id_type=MESH)

    loads = []
    for i in range(NB):
        rows = pl.ds(pl.multiple_of(HM + at_b(i) * BL, 256), BL)
        loads.append(pltpu.make_async_copy(f_hbm.at[0, rows, :], fown.at[i], f_sem.at[i]))
    for side in range(2):
        rows = pl.ds(side * (HM + NB * BL), HM)
        loads.append(pltpu.make_async_copy(f_hbm.at[0, rows, :], fmar.at[side], g_sem.at[side]))
    mloads = {}
    for k, d in enumerate(Z_ORDER):
        for l in range(NY):
            cols = pl.ds(pl.multiple_of(l * (NZ * CS) + zpos(NZ - d) * CS, 256), CS)
            mloads[k, l] = pltpu.make_async_copy(m_hbm.at[:, 0, cols], mbuf.at[k, l], m_sem.at[k, l])
    loads[0].start()
    for k in range(NZ):
        for l in range(NY):
            mloads[k, l].start()
    for c in loads[1:]:
        c.start()

    low_half = lax.broadcasted_iota(jnp.int32, (PR // 2, 128), 1) < 64

    def halves(even, odd):
        return jnp.where(low_half, even, pltpu.roll(odd, 64, 1)), jnp.where(low_half, pltpu.roll(even, 64, 1), odd)

    onehot = (lax.broadcasted_iota(jnp.int32, (CS, BL), 0) == agg_ref[...]).astype(BF16)
    part = exact(res_ref[...], onehot, NT)
    for h in range(2):
        wide = part[:, h * 128 : (h + 1) * 128]
        even, odd = halves(wide[: PR // 2], wide[PR // 2 :])
        qout[2 * h] = even
        qout[2 * h + 1] = odd

    pl.semaphore_wait(barrier, len(partners))

    def remote(src, dst, ss, rs, to):
        return pltpu.make_async_remote_copy(
            src_ref=src, dst_ref=dst, send_sem=ss, recv_sem=rs, device_id=to, device_id_type=MESH
        )

    sent = []

    def send(*args):
        c = remote(*args)
        c.start()
        sent.append(c)

    ydesc = {}
    for other in range(2):
        for i in range(NB):
            if other or i:
                to = at_b(NB - i)
                args = (qout.at[to], ybuf.at[other, i], y_s.at[other, i], y_r.at[other, i], (mate if other else s, to))
                ydesc[other, i] = args
                send(*args)
    wdesc = [
        (want_ref, nwant.at[0], w_s.at[0], w_r.at[0], (nxt, b)),
        (want_ref, nwant.at[1], w_s.at[1], w_r.at[1], (prv, b)),
    ]
    for args in wdesc:
        send(*args)
    odesc = {}
    for i in range(1, NB):
        args = (res_ref, own.at[i - 1], own_s.at[i], own_r.at[i], (s, at_b(NB - i)))
        odesc[i] = args
        send(*args)

    loads[0].wait()
    fine = three(res_ref[...], fown[0])

    for key in ydesc:
        remote(*ydesc[key]).wait_recv()
    mine = (qout[b] + ybuf[0, 1]) + (ybuf[0, 2] + ybuf[0, 3])
    theirs = (ybuf[1, 0] + ybuf[1, 1]) + (ybuf[1, 2] + ybuf[1, 3])
    slot = z * NX + x
    xg[slot, pl.ds(pl.multiple_of(yl * 16, 16), 16), :] = mine
    xg[slot, pl.ds(pl.multiple_of((1 - yl) * 16, 16), 16), :] = theirs

    def forward(k, d):
        here = zpos(NZ - d) * NX + x
        for e in (1, 3, 2):
            send(xg.at[here], xg.at[here], x_s.at[k, e], x_r.at[k, e], (at_x(e), b))

    for d in Z_ORDER[1:]:
        send(xg.at[slot], xg.at[slot], z_s.at[d], z_r.at[d], (at_z(d), b))
    forward(0, 0)

    for i in range(1, NB):
        loads[i].wait()
        remote(*odesc[i]).wait_recv()
        fine += three(own[i - 1], fown[i])
    for k in (0, 1):
        remote(*wdesc[k]).wait_recv()

    def margin(side):
        wanted = nwant[side, 0, 1 - side : 2 - side, :]
        total = jnp.zeros((PR, HM), F32)
        for i in range(NB):
            rows = lax.broadcasted_iota(jnp.int32, (BL, HM), 0) + at_b(i) * BL
            total += exact(res_ref[...] if i == 0 else own[i - 1], (rows == wanted).astype(BF16))
        hout[side] = total

    hdesc = [
        (hout.at[0], hin.at[1], h_s.at[0], h_r.at[1], (prv, b)),
        (hout.at[1], hin.at[0], h_s.at[1], h_r.at[0], (nxt, b)),
    ]

    def await_z(k):
        d = Z_ORDER[k]
        here = xg.at[zpos(NZ - d) * NX + x]
        remote(here, here, z_s.at[d], z_r.at[d], (at_z(d), b)).wait_recv()
        forward(k, d)

    def product(k):
        d = Z_ORDER[k]
        base = zpos(NZ - d) * NX
        for e in (1, 3, 2):
            there = xg.at[base + lax.rem(x + NX - e, NX)]
            remote(there, there, x_s.at[k, e], x_r.at[k, e], (at_x(e), b)).wait_recv()
        total = None
        for l in range(NY):
            cols = []
            for h in range(2):
                even = xg[base + 2 * h, 16 * l : 16 * l + 16, :]
                odd = xg[base + 2 * h + 1, 16 * l : 16 * l + 16, :]
                top, bottom = halves(even, odd)
                cols.append(jnp.concatenate([top, bottom], axis=0))
            mloads[k, l].wait()
            r = three(jnp.concatenate(cols, axis=1), mbuf[k, l], NT)
            total = r if total is None else total + r
        return total

    await_z(1)
    await_z(2)
    margin(0)
    send(*hdesc[0])
    await_z(3)
    await_z(4)
    margin(1)
    send(*hdesc[1])
    await_z(5)
    await_z(6)
    coarse = product(0)
    await_z(7)
    for k in range(1, NZ):
        coarse += product(k)

    ysum[0] = coarse
    adesc = {}
    for i in range(1, NB):
        args = (ysum.at[0], ysum.at[i], a_s.at[i], a_r.at[i], (s, at_b(NB - i)))
        adesc[i] = args
        send(*args)

    slots = lax.broadcasted_iota(jnp.int32, (PR, HM), 1)
    for side in range(2):
        remote(*hdesc[1 - side]).wait_recv()
        edge = s == (0 if side == 0 else NSUB - 1)
        kept = jnp.where(edge, 0, count_ref[0, side])
        loads[NB + side].wait()
        fine += three(jnp.where(slots < kept, hin[side], 0.0), fmar[side])

    for i in range(1, NB):
        remote(*adesc[i]).wait_recv()
    coarse = (ysum[0] + ysum[1]) + (ysum[2] + ysum[3])
    out_ref[...] = fine + exact(coarse, onehot)
    for c in sent:
        c.wait_send()


def on_device(residual, fine_inverse, coarse_inverse, wanted_rows, wanted_count, aggregate):
    vmem = pl.BlockSpec(memory_space=pltpu.VMEM)
    hbm = pl.BlockSpec(memory_space=pltpu.HBM)
    dma = pltpu.SemaphoreType.DMA
    return pl.pallas_call(
        kernel,
        out_shape=jax.ShapeDtypeStruct((PR, BL), F32),
        in_specs=[vmem, vmem, vmem, pl.BlockSpec(memory_space=pltpu.SMEM), hbm, hbm],
        out_specs=vmem,
        scratch_shapes=[
            pltpu.VMEM((NZ, NY, CS, CS), F32),
            pltpu.VMEM((NB, BL, BL), F32),
            pltpu.VMEM((2, HM, BL), F32),
            pltpu.VMEM((NB - 1, PR, BL), F32),
            pltpu.VMEM((NB, PR // 2, 128), F32),
            pltpu.VMEM((2, NB, PR // 2, 128), F32),
            pltpu.VMEM((NZ * NX, PR, 128), F32),
            pltpu.VMEM((2, 1, 2, HM), jnp.int32),
            pltpu.VMEM((2, PR, HM), F32),
            pltpu.VMEM((2, PR, HM), F32),
            pltpu.VMEM((NB, PR, CS), F32),
            dma((NZ, NY)), dma((NB,)), dma((2,)),
            dma((NB,)), dma((NB,)),
            dma((2, NB)), dma((2, NB)),
            dma((NZ,)), dma((NZ,)),
            dma((NZ, NX)), dma((NZ, NX)),
            dma((2,)), dma((2,)),
            dma((2,)), dma((2,)),
            dma((NB,)), dma((NB,)),
        ],
        compiler_params=pltpu.CompilerParams(
            collective_id=0, has_side_effects=True, vmem_limit_bytes=48 * 1024 * 1024
        ),
        name="schwarz",
    )(residual, aggregate.reshape(1, BL), wanted_rows, wanted_count, coarse_inverse, fine_inverse)


def solution(mesh):
    in_specs = (
        P(None, ("sub", "blk")),
        P("sub", None, "blk"),
        P("sub", "blk", None),
        P("sub", None, None),
        P("sub", None),
        P(("sub", "blk")),
    )
    out_specs = P(None, ("sub", "blk"))
    return jax.shard_map(
        on_device, mesh=mesh, in_specs=in_specs, out_specs=out_specs, check_vma=False
    )
```

```python
import jax
import jax.numpy as jnp
from jax import lax
from jax.experimental import pallas as pl
from jax.experimental.pallas import tpu as pltpu
from jax.sharding import PartitionSpec as P

NX, NZ, NY = 4, 8, 2
NB = 4
NSUB = NX * NZ * NY
PR = 32
BL = 512
CS = 256
HM = 256
F32, BF16 = jnp.float32, jnp.bfloat16
MESH = pl.DeviceIdType.MESH
Z_ORDER = (0, 1, 7, 2, 6, 3, 5, 4)
NEAR = (1, 7, 2, 6)
NN = (((1,), (0,)), ((), ()))
NT = (((1,), (1,)), ((), ()))


def mm(a, b, dims=NN):
    return lax.dot_general(a, b, dims, preferred_element_type=F32)


def split2(v):
    hi = v.astype(BF16)
    return hi, (v - hi.astype(F32)).astype(BF16)


def split3(v):
    hi = v.astype(BF16)
    rest = v - hi.astype(F32)
    mid = rest.astype(BF16)
    return hi, mid, (rest - mid.astype(F32)).astype(BF16)


def exact(v, onehot, dims=NN):
    n = v.shape[0]
    r = mm(jnp.concatenate(split3(v), axis=0), onehot, dims)
    return (r[:n] + r[n : 2 * n]) + r[2 * n :]


def three(v, w, dims=NN):
    n = v.shape[0]
    vh, vl = split2(v)
    wh, wl = split2(w)
    r = mm(jnp.concatenate([vh, vl], axis=0), wh, dims)
    return (r[:n] + r[n:]) + mm(vh, wl, dims)


def kernel(
    res_hbm, agg_hbm, want_hbm, count_hbm, m_hbm, f_hbm, out_ref,
    res_ref, agg_ref, want_ref, count_ref, mbuf, fown, fmar, own, qout, ybuf, xg, nwant, hout, hin, ysum,
    i_sem, m_sem, f_sem, g_sem, own_s, own_r, y_s, y_r, z_s, z_r, v_s, v_r, x_s, x_r, w_s, w_r, h_s, h_r, a_s, a_r, far,
):
    s = lax.axis_index("sub")
    b = lax.axis_index("blk")
    yl = s // (NZ * NX)
    z = lax.rem(s // NX, NZ)
    x = lax.rem(s, NX)
    mate = lax.rem(s + NZ * NX, NSUB)

    def zpos(d):
        return lax.rem(z + d, NZ)

    def at_z(d):
        return yl * (NZ * NX) + zpos(d) * NX + x

    def at_x(d):
        return s - x + lax.rem(x + d, NX)

    at_b = (b, b + 1 - 2 * lax.rem(b, 2), lax.rem(b + 2, NB), NB - 1 - b)
    nxt, prv = lax.rem(s + 1, NSUB), lax.rem(s + NSUB - 1, NSUB)

    partners = [(s, at_b[i]) for i in (2, 3, 1)] + [(mate, at_b[i]) for i in range(NB)]
    partners += [(at_z(d), b) for d in (2, 6, 1, 7)] + [(at_x(d), b) for d in (2, 1, 3)]
    partners += [(nxt, b), (prv, b)]
    barrier = pltpu.get_barrier_semaphore()
    for p in partners:
        pl.semaphore_signal(barrier, inc=1, device_id=p, device_id_type=MESH)

    inputs = [
        pltpu.make_async_copy(src, dst, i_sem.at[i])
        for i, (src, dst) in enumerate(
            [(res_hbm, res_ref), (agg_hbm, agg_ref), (want_hbm, want_ref), (count_hbm, count_ref)]
        )
    ]
    for c in inputs:
        c.start()

    loads = []
    for i in range(NB):
        rows = pl.ds(pl.multiple_of(HM + at_b[i] * BL, 256), BL)
        loads.append(pltpu.make_async_copy(f_hbm.at[0, rows, :], fown.at[i], f_sem.at[i]))
    for side in range(2):
        rows = pl.ds(side * (HM + NB * BL), HM)
        loads.append(pltpu.make_async_copy(f_hbm.at[0, rows, :], fmar.at[side], g_sem.at[side]))
    mloads = {}
    for d in Z_ORDER:
        for l in range(NY):
            cols = pl.ds(pl.multiple_of(l * (NZ * CS) + zpos(NZ - d) * CS, 256), CS)
            mloads[d, l] = pltpu.make_async_copy(m_hbm.at[:, 0, cols], mbuf.at[d, l], m_sem.at[d, l])
    loads[0].start()
    for c in mloads.values():
        c.start()
    for c in loads[1:]:
        c.start()

    low_half = lax.broadcasted_iota(jnp.int32, (PR // 2, 128), 1) < 64

    def halves(even, odd):
        return jnp.where(low_half, even, pltpu.roll(odd, 64, 1)), jnp.where(low_half, pltpu.roll(even, 64, 1), odd)

    inputs[0].wait()
    inputs[1].wait()
    onehot = (lax.broadcasted_iota(jnp.int32, (CS, BL), 0) == agg_ref[...]).astype(BF16)
    part = exact(res_ref[...], onehot, NT)
    for h in range(2):
        wide = part[:, h * 128 : (h + 1) * 128]
        even, odd = halves(wide[: PR // 2], wide[PR // 2 :])
        qout[2 * h] = even
        qout[2 * h + 1] = odd

    pl.semaphore_wait(barrier, len(partners))

    def remote(src, dst, ss, rs, to):
        return pltpu.make_async_remote_copy(
            src_ref=src, dst_ref=dst, send_sem=ss, recv_sem=rs, device_id=to, device_id_type=MESH
        )

    sent = []

    def send(*args):
        c = remote(*args)
        c.start()
        sent.append(c)

    ydesc = []
    for other, i in ((0, 2), (0, 3), (1, 0), (1, 1), (1, 2), (1, 3), (0, 1)):
        to = at_b[i]
        ydesc.append((qout.at[to], ybuf.at[other, i], y_s.at[other, i], y_r.at[other, i], (mate if other else s, to)))
        send(*ydesc[-1])
    for d in (2, 6):
        pl.semaphore_signal(far, inc=1, device_id=(at_z(d), b), device_id_type=MESH)
    inputs[2].wait()
    wdesc = [
        (want_ref, nwant.at[0], w_s.at[0], w_r.at[0], (nxt, b)),
        (want_ref, nwant.at[1], w_s.at[1], w_r.at[1], (prv, b)),
    ]
    for args in wdesc:
        send(*args)

    loads[0].wait()
    fine = three(res_ref[...], fown[0])

    for args in ydesc:
        remote(*args).wait_recv()
    mine = (qout[b] + ybuf[0, 1]) + (ybuf[0, 2] + ybuf[0, 3])
    theirs = (ybuf[1, 0] + ybuf[1, 1]) + (ybuf[1, 2] + ybuf[1, 3])
    slot = z * NX + x
    xg[slot, pl.ds(pl.multiple_of(yl * 16, 16), 16), :] = mine
    xg[slot, pl.ds(pl.multiple_of((1 - yl) * 16, 16), 16), :] = theirs

    def slot_of(d, e):
        return zpos(NZ - d) * NX + lax.rem(x + NX - e, NX)

    def to_z(d, e, ss, rs):
        here = xg.at[z * NX + lax.rem(x + NX - e, NX)]
        send(here, here, ss.at[d], rs.at[d], (at_z(d), b))

    def to_x(d):
        here = xg.at[slot_of(d, 0)]
        for e in (1, 3) if d in NEAR else (2, 1, 3):
            send(here, here, x_s.at[d, e], x_r.at[d, e], (at_x(e), b))

    def await_block(d, e, ss, rs):
        there = xg.at[slot_of(d, e)]
        remote(there, there, ss, rs, (s, at_b[1])).wait_recv()

    def await_z(*ds):
        for d in ds:
            await_block(d, 0, z_s.at[d], z_r.at[d])
            to_x(d)

    for d in (1, 7):
        to_z(d, 0, z_s, z_r)
    to_x(0)
    for d in (2, 6):
        to_z(d, 0, z_s, z_r)
    pl.semaphore_wait(far, 2)
    for d in (4, 3, 5):
        to_z(d, 0, z_s, z_r)
    odesc = {}
    for i in (2, 3, 1):
        odesc[i] = (res_ref, own.at[i - 1], own_s.at[i], own_r.at[i], (s, at_b[i]))
        send(*odesc[i])

    await_z(1, 7)
    await_z(2, 6)
    await_block(0, 2, x_s.at[0, 2], x_r.at[0, 2])
    for d in NEAR:
        to_z(d, 2, v_s, v_r)
    await_z(3, 5)
    await_z(4)

    def products(*ds):
        for d in ds:
            for e in (1, 3) if d in NEAR else (1, 3) if d == 0 else (1, 3, 2):
                await_block(d, e, x_s.at[d, e], x_r.at[d, e])
            if d in NEAR:
                await_block(d, 2, v_s.at[d], v_r.at[d])
            for l in range(NY):
                mloads[d, l].wait()
        total = None
        for d in ds:
            base = zpos(NZ - d) * NX
            for l in range(NY):
                cols = []
                for h in range(2):
                    even = xg[base + 2 * h, 16 * l : 16 * l + 16, :]
                    odd = xg[base + 2 * h + 1, 16 * l : 16 * l + 16, :]
                    cols.append(jnp.concatenate(halves(even, odd), axis=0))
                r = three(jnp.concatenate(cols, axis=1), mbuf[d, l], NT)
                total = r if total is None else total + r
        return total

    coarse = products(0, 1, 7)
    coarse += products(2, 6)

    for i in (2, 3, 1):
        remote(*odesc[i]).wait_recv()
    for args in wdesc:
        remote(*args).wait_recv()
    hdesc = [
        (hout.at[0], hin.at[1], h_s.at[0], h_r.at[1], (prv, b)),
        (hout.at[1], hin.at[0], h_s.at[1], h_r.at[0], (nxt, b)),
    ]
    for side in range(2):
        wanted = nwant[side, 0, 1 - side : 2 - side, :]
        total = None
        for i in range(NB):
            rows = lax.broadcasted_iota(jnp.int32, (BL, HM), 0) + at_b[i] * BL
            r = exact(res_ref[...] if i == 0 else own[i - 1], (rows == wanted).astype(BF16))
            total = r if total is None else total + r
        hout[side] = total
    for args in hdesc:
        send(*args)

    coarse += products(3, 5, 4)
    ysum[0] = coarse
    adesc = {}
    for i in (2, 3, 1):
        adesc[i] = (ysum.at[0], ysum.at[i], a_s.at[i], a_r.at[i], (s, at_b[i]))
        send(*adesc[i])

    for i in range(1, NB):
        loads[i].wait()
    for i in range(1, NB):
        fine += three(own[i - 1], fown[i])
    inputs[3].wait()
    slots = lax.broadcasted_iota(jnp.int32, (PR, HM), 1)
    for side in range(2):
        remote(*hdesc[1 - side]).wait_recv()
        loads[NB + side].wait()
    for side in range(2):
        edge = s == (0 if side == 0 else NSUB - 1)
        kept = jnp.where(edge, 0, count_ref[0, side])
        fine += three(jnp.where(slots < kept, hin[side], 0.0), fmar[side])

    for i in (1, 2, 3):
        remote(*adesc[i]).wait_recv()
    coarse = (ysum[0] + ysum[1]) + (ysum[2] + ysum[3])
    out_ref[...] = fine + exact(coarse, onehot)
    for c in sent:
        c.wait_send()


def on_device(residual, fine_inverse, coarse_inverse, wanted_rows, wanted_count, aggregate):
    vmem = pl.BlockSpec(memory_space=pltpu.VMEM)
    hbm = pl.BlockSpec(memory_space=pl.ANY)
    dma = pltpu.SemaphoreType.DMA
    return pl.pallas_call(
        kernel,
        out_shape=jax.ShapeDtypeStruct((PR, BL), F32),
        in_specs=[hbm] * 6,
        out_specs=vmem,
        scratch_shapes=[
            pltpu.VMEM((PR, BL), F32),
            pltpu.VMEM((1, BL), jnp.int32),
            pltpu.VMEM((1, 2, HM), jnp.int32),
            pltpu.SMEM((1, 2), jnp.int32),
            pltpu.VMEM((NZ, NY, CS, CS), F32),
            pltpu.VMEM((NB, BL, BL), F32),
            pltpu.VMEM((2, HM, BL), F32),
            pltpu.VMEM((NB - 1, PR, BL), F32),
            pltpu.VMEM((NB, PR // 2, 128), F32),
            pltpu.VMEM((2, NB, PR // 2, 128), F32),
            pltpu.VMEM((NZ * NX, PR, 128), F32),
            pltpu.VMEM((2, 1, 2, HM), jnp.int32),
            pltpu.VMEM((2, PR, HM), F32),
            pltpu.VMEM((2, PR, HM), F32),
            pltpu.VMEM((NB, PR, CS), F32),
            dma((4,)), dma((NZ, NY)), dma((NB,)), dma((2,)),
            dma((NB,)), dma((NB,)),
            dma((2, NB)), dma((2, NB)),
            dma((NZ,)), dma((NZ,)),
            dma((NZ,)), dma((NZ,)),
            dma((NZ, NX)), dma((NZ, NX)),
            dma((2,)), dma((2,)),
            dma((2,)), dma((2,)),
            dma((NB,)), dma((NB,)),
            pltpu.SemaphoreType.REGULAR,
        ],
        compiler_params=pltpu.CompilerParams(
            collective_id=0, has_side_effects=True, vmem_limit_bytes=48 * 1024 * 1024
        ),
        name="schwarz",
    )(*[pltpu.with_memory_space_constraint(v, pltpu.HBM) for v in (residual, aggregate.reshape(1, BL), wanted_rows, wanted_count, coarse_inverse, fine_inverse)])


def solution(mesh):
    in_specs = (
        P(None, ("sub", "blk")),
        P("sub", None, "blk"),
        P("sub", "blk", None),
        P("sub", None, None),
        P("sub", None),
        P(("sub", "blk")),
    )
    out_specs = P(None, ("sub", "blk"))
    return jax.shard_map(
        on_device, mesh=mesh, in_specs=in_specs, out_specs=out_specs, check_vma=False
    )
```

```python
import jax
import jax.numpy as jnp
from jax import lax
from jax.experimental import pallas as pl
from jax.experimental.pallas import tpu as pltpu
from jax.sharding import PartitionSpec as P

NX, NZ, NY = 4, 8, 2
NB = 4
NSUB = NX * NZ * NY
PR = 32
BL = 512
CS = 256
HM = 256
F32, BF16 = jnp.float32, jnp.bfloat16
MESH = pl.DeviceIdType.MESH
EARLY, LATE = (0, 1, 2, 3), (7, 6, 5, 4)
NEAR = (1, 2, 7, 6)
NN = (((1,), (0,)), ((), ()))
NT = (((1,), (1,)), ((), ()))


def mm(a, b, dims=NN):
    return lax.dot_general(a, b, dims, preferred_element_type=F32)


def split2(v):
    hi = v.astype(BF16)
    return hi, (v - hi.astype(F32)).astype(BF16)


def split3(v):
    hi = v.astype(BF16)
    rest = v - hi.astype(F32)
    mid = rest.astype(BF16)
    return hi, mid, (rest - mid.astype(F32)).astype(BF16)


def exact(v, onehot, dims=NN):
    n = v.shape[0]
    r = mm(jnp.concatenate(split3(v), axis=0), onehot, dims)
    return (r[:n] + r[n : 2 * n]) + r[2 * n :]


def three(v, w, dims=NN):
    n = v.shape[0]
    vh, vl = split2(v)
    wh, wl = split2(w)
    r = mm(jnp.concatenate([vh, vl], axis=0), wh, dims)
    return (r[:n] + r[n:]) + mm(vh, wl, dims)


def kernel(
    res_hbm, agg_hbm, want_hbm, count_hbm, m_hbm, f_hbm, out_ref,
    res_ref, agg_ref, want_ref, count_ref, mbuf, fown, fmar, own, qout, ybuf, xg, nwant, hout, hin, ysum,
    i_sem, m_sem, f_sem, g_sem, own_s, own_r, y_s, y_r, z_s, z_r, v_s, o_r, x_s, x_r, w_s, w_r, h_s, h_r, a_s, a_r, z_in, s_in,
):
    s = lax.axis_index("sub")
    b = lax.axis_index("blk")
    yl = s // (NZ * NX)
    z = lax.rem(s // NX, NZ)
    x = lax.rem(s, NX)
    mate = lax.rem(s + NZ * NX, NSUB)

    def zpos(d):
        return lax.rem(z + d, NZ)

    def at_z(d):
        return yl * (NZ * NX) + zpos(d) * NX + x

    def at_x(d):
        return s - x + lax.rem(x + d, NX)

    at_b = (b, b + 1 - 2 * lax.rem(b, 2), lax.rem(b + 2, NB), NB - 1 - b)
    nxt, prv = lax.rem(s + 1, NSUB), lax.rem(s + NSUB - 1, NSUB)

    inputs = [
        pltpu.make_async_copy(src, dst, i_sem.at[i])
        for i, (src, dst) in enumerate(
            [(res_hbm, res_ref), (agg_hbm, agg_ref), (want_hbm, want_ref), (count_hbm, count_ref)]
        )
    ]
    for c in inputs:
        c.start()

    def along_z(zp):
        return (yl * (NZ * NX) + zp * NX + x, b)

    cross_next, cross_prev = x == NX - 1, x == 0
    barrier = pltpu.get_barrier_semaphore()

    def signal(sem, to):
        pl.semaphore_signal(sem, inc=1, device_id=to, device_id_type=MESH)

    level = [(s, at_b[i]) for i in (2, 3, 1)] + [(mate, at_b[i]) for i in range(NB)] + [(at_x(d), b) for d in (2, 1, 3)]
    for p in level:
        signal(barrier, p)
    for zp in range(1, NZ):
        @pl.when(zp > z)
        def _():
            signal(barrier, along_z(zp))

    @pl.when(cross_next & (z < NZ - 1))
    def _():
        signal(barrier, (nxt, b))

    @pl.when(cross_prev & (z == 0))
    def _():
        signal(barrier, (prv, b))

    answers_prev, answers_next = cross_prev & (z > 0), cross_next & (z == NZ - 1)
    greeted = len(level) + z + jnp.where(answers_prev | answers_next, 1, 0)

    low_half = lax.broadcasted_iota(jnp.int32, (PR // 2, 128), 1) < 64

    def halves(even, odd):
        return jnp.where(low_half, even, pltpu.roll(odd, 64, 1)), jnp.where(low_half, pltpu.roll(even, 64, 1), odd)

    inputs[0].wait()
    inputs[1].wait()
    onehot = (lax.broadcasted_iota(jnp.int32, (CS, BL), 0) == agg_ref[...]).astype(BF16)
    part = exact(res_ref[...], onehot, NT)
    for h in range(2):
        wide = part[:, h * 128 : (h + 1) * 128]
        even, odd = halves(wide[: PR // 2], wide[PR // 2 :])
        qout[2 * h] = even
        qout[2 * h + 1] = odd

    pl.semaphore_wait(barrier, greeted)

    def remote(src, dst, ss, rs, to):
        return pltpu.make_async_remote_copy(
            src_ref=src, dst_ref=dst, send_sem=ss, recv_sem=rs, device_id=to, device_id_type=MESH
        )

    sent = []

    def send(*args):
        c = remote(*args)
        c.start()
        sent.append(c)

    ydesc = []
    for other, i in ((0, 2), (0, 3), (1, 0), (1, 1), (1, 2), (1, 3), (0, 1)):
        to = at_b[i]
        ydesc.append((qout.at[to], ybuf.at[other, i], y_s.at[other, i], y_r.at[other, i], (mate if other else s, to)))
        send(*ydesc[-1])
    for zp in range(NZ - 1):
        @pl.when(zp < z)
        def _():
            signal(z_in.at[z], along_z(zp))

    @pl.when(answers_prev)
    def _():
        signal(s_in, (prv, b))

    @pl.when(answers_next)
    def _():
        signal(s_in, (nxt, b))

    loads = []
    for i in range(NB):
        rows = pl.ds(pl.multiple_of(HM + at_b[i] * BL, 256), BL)
        loads.append(pltpu.make_async_copy(f_hbm.at[0, rows, :], fown.at[i], f_sem.at[i]))
    for side in range(2):
        rows = pl.ds(side * (HM + NB * BL), HM)
        loads.append(pltpu.make_async_copy(f_hbm.at[0, rows, :], fmar.at[side], g_sem.at[side]))
    for c in loads:
        c.start()
    mloads = {}
    for zp in range(NZ):
        for l in range(NY):
            cols = pl.ds(l * (NZ * CS) + zp * CS, CS)
            mloads[zp, l] = pltpu.make_async_copy(m_hbm.at[:, 0, cols], mbuf.at[zp, l], m_sem.at[zp, l])
            mloads[zp, l].start()
    loads[0].wait()
    fine = three(res_ref[...], fown[0])

    for args in ydesc:
        remote(*args).wait_recv()
    mine = (qout[b] + ybuf[0, 1]) + (ybuf[0, 2] + ybuf[0, 3])
    theirs = (ybuf[1, 0] + ybuf[1, 1]) + (ybuf[1, 2] + ybuf[1, 3])
    slot = z * NX + x
    xg[slot, pl.ds(pl.multiple_of(yl * 16, 16), 16), :] = mine
    xg[slot, pl.ds(pl.multiple_of((1 - yl) * 16, 16), 16), :] = theirs

    def block(zp, e):
        return xg.at[zp * NX + lax.rem(x + NX - e, NX)]

    def near(zp):
        d = lax.rem(z + NZ - zp, NZ)
        return (d == 1) | (d == 2) | (d == 6) | (d == 7)

    def z_copy(zp):
        return remote(block(z, 0), block(z, 0), z_s.at[zp], z_r.at[z], along_z(zp))

    def v_copy(d):
        return remote(block(z, 2), block(z, 2), v_s.at[d], o_r.at[z], (at_z(d), b))

    def x_copy(zp, e):
        rs = o_r.at[zp] if e == 2 else x_r.at[zp, e]
        return remote(block(zp, 0), block(zp, 0), x_s.at[zp, e], rs, (at_x(e), b))

    def arrival(zp, e, rs):
        remote(block(zp, e), block(zp, e), x_s.at[0, 0], rs, (s, at_b[1])).wait_recv()

    def forward(zp):
        @pl.when(zp != z)
        def _():
            arrival(zp, 0, z_r.at[zp])

            @pl.when(jnp.logical_not(near(zp)))
            def _():
                x_copy(zp, 2).start()

            x_copy(zp, 1).start()
            x_copy(zp, 3).start()

    for zp in range(NZ - 1):
        @pl.when(zp < z)
        def _():
            z_copy(zp).start()
    for e in (2, 1, 3):
        x_copy(z, e).start()
    odesc = {}
    for i in (2, 3, 1):
        odesc[i] = (res_ref, own.at[i - 1], own_s.at[i], own_r.at[i], (s, at_b[i]))
        send(*odesc[i])
    for zp in range(1, NZ):
        @pl.when(zp > z)
        def _():
            pl.semaphore_wait(z_in.at[zp], 1)
            z_copy(zp).start()
    inputs[2].wait()

    @pl.when((cross_next & (z < NZ - 1)) | (cross_prev & (z == 0)))
    def _():
        pl.semaphore_wait(s_in, 1)

    wdesc = [
        (want_ref, nwant.at[0], w_s.at[0], w_r.at[0], (nxt, b)),
        (want_ref, nwant.at[1], w_s.at[1], w_r.at[1], (prv, b)),
    ]
    for args in wdesc:
        send(*args)
    hdesc = [
        (hout.at[0], hin.at[1], h_s.at[0], h_r.at[1], (prv, b)),
        (hout.at[1], hin.at[0], h_s.at[1], h_r.at[0], (nxt, b)),
    ]

    for zp in EARLY:
        forward(zp)
    arrival(z, 2, o_r.at[z])
    for d in NEAR:
        v_copy(d).start()

    def margin(side):
        remote(*wdesc[side]).wait_recv()
        wanted = nwant[side, 0, 1 - side : 2 - side, :]
        total = None
        for i in range(NB):
            rows = lax.broadcasted_iota(jnp.int32, (BL, HM), 0) + at_b[i] * BL
            r = exact(res_ref[...] if i == 0 else own[i - 1], (rows == wanted).astype(BF16))
            total = r if total is None else total + r
        hout[side] = total
        remote(*hdesc[side]).start()

    late_prev = cross_prev & (z == 0)
    for i in (2, 3, 1):
        remote(*odesc[i]).wait_recv()
    margin(1)

    @pl.when(jnp.logical_not(late_prev))
    def _():
        margin(0)

    def products(*zps):
        for zp in zps:
            for e in (1, 3):
                arrival(zp, e, x_r.at[zp, e])

            @pl.when(zp != z)
            def _():
                arrival(zp, 2, o_r.at[zp])

            for l in range(NY):
                mloads[zp, l].wait()
        total = None
        for zp in zps:
            for l in range(NY):
                cols = []
                for h in range(2):
                    even = xg[zp * NX + 2 * h, 16 * l : 16 * l + 16, :]
                    odd = xg[zp * NX + 2 * h + 1, 16 * l : 16 * l + 16, :]
                    cols.append(jnp.concatenate(halves(even, odd), axis=0))
                r = three(jnp.concatenate(cols, axis=1), mbuf[zp, l], NT)
                total = r if total is None else total + r
        return total

    for zp in LATE:
        forward(zp)

    @pl.when(late_prev)
    def _():
        margin(0)

    coarse = products(*EARLY)
    coarse += products(*LATE[:2])
    coarse += products(*LATE[2:])
    ysum[0] = coarse
    adesc = {}
    for i in (2, 3, 1):
        adesc[i] = (ysum.at[0], ysum.at[i], a_s.at[i], a_r.at[i], (s, at_b[i]))
        send(*adesc[i])

    for i in range(1, NB):
        loads[i].wait()
    for i in range(1, NB):
        fine += three(own[i - 1], fown[i])
    inputs[3].wait()
    slots = lax.broadcasted_iota(jnp.int32, (PR, HM), 1)
    for side in range(2):
        remote(*hdesc[1 - side]).wait_recv()
        loads[NB + side].wait()
    for side in range(2):
        edge = s == (0 if side == 0 else NSUB - 1)
        kept = jnp.where(edge, 0, count_ref[0, side])
        fine += three(jnp.where(slots < kept, hin[side], 0.0), fmar[side])

    for i in (1, 2, 3):
        remote(*adesc[i]).wait_recv()
    coarse = (ysum[0] + ysum[1]) + (ysum[2] + ysum[3])
    out_ref[...] = fine + exact(coarse, onehot)
    for c in sent + [remote(*args) for args in hdesc]:
        c.wait_send()
    for zp in range(NZ):
        @pl.when(zp != z)
        def _():
            z_copy(zp).wait_send()

        @pl.when(jnp.logical_not(near(zp)))
        def _():
            x_copy(zp, 2).wait_send()

        x_copy(zp, 1).wait_send()
        x_copy(zp, 3).wait_send()
    for d in NEAR:
        v_copy(d).wait_send()


def on_device(residual, fine_inverse, coarse_inverse, wanted_rows, wanted_count, aggregate):
    vmem = pl.BlockSpec(memory_space=pltpu.VMEM)
    hbm = pl.BlockSpec(memory_space=pl.ANY)
    dma = pltpu.SemaphoreType.DMA
    return pl.pallas_call(
        kernel,
        out_shape=jax.ShapeDtypeStruct((PR, BL), F32),
        in_specs=[hbm] * 6,
        out_specs=vmem,
        scratch_shapes=[
            pltpu.VMEM((PR, BL), F32),
            pltpu.VMEM((1, BL), jnp.int32),
            pltpu.VMEM((1, 2, HM), jnp.int32),
            pltpu.SMEM((1, 2), jnp.int32),
            pltpu.VMEM((NZ, NY, CS, CS), F32),
            pltpu.VMEM((NB, BL, BL), F32),
            pltpu.VMEM((2, HM, BL), F32),
            pltpu.VMEM((NB - 1, PR, BL), F32),
            pltpu.VMEM((NB, PR // 2, 128), F32),
            pltpu.VMEM((2, NB, PR // 2, 128), F32),
            pltpu.VMEM((NZ * NX, PR, 128), F32),
            pltpu.VMEM((2, 1, 2, HM), jnp.int32),
            pltpu.VMEM((2, PR, HM), F32),
            pltpu.VMEM((2, PR, HM), F32),
            pltpu.VMEM((NB, PR, CS), F32),
            dma((4,)), dma((NZ, NY)), dma((NB,)), dma((2,)),
            dma((NB,)), dma((NB,)),
            dma((2, NB)), dma((2, NB)),
            dma((NZ,)), dma((NZ,)),
            dma((NZ,)), dma((NZ,)),
            dma((NZ, NX)), dma((NZ, NX)),
            dma((2,)), dma((2,)),
            dma((2,)), dma((2,)),
            dma((NB,)), dma((NB,)),
            pltpu.SemaphoreType.REGULAR((NZ,)), pltpu.SemaphoreType.REGULAR,
        ],
        compiler_params=pltpu.CompilerParams(
            collective_id=0, has_side_effects=True, vmem_limit_bytes=48 * 1024 * 1024
        ),
        name="schwarz",
    )(*[pltpu.with_memory_space_constraint(v, pltpu.HBM) for v in (residual, aggregate.reshape(1, BL), wanted_rows, wanted_count, coarse_inverse, fine_inverse)])


def solution(mesh):
    in_specs = (
        P(None, ("sub", "blk")),
        P("sub", None, "blk"),
        P("sub", "blk", None),
        P("sub", None, None),
        P("sub", None),
        P(("sub", "blk")),
    )
    out_specs = P(None, ("sub", "blk"))
    return jax.shard_map(
        on_device, mesh=mesh, in_specs=in_specs, out_specs=out_specs, check_vma=False
    )
```

```python
import jax
import jax.numpy as jnp
from jax import lax
from jax.experimental import pallas as pl
from jax.experimental.pallas import tpu as pltpu
from jax.sharding import PartitionSpec as P

NX, NZ, NY = 4, 8, 2
NB = 4
NSUB = NX * NZ * NY
PR = 32
BL = 512
CS = 256
HM = 256
F32, BF16 = jnp.float32, jnp.bfloat16
MESH = pl.DeviceIdType.MESH
EARLY, LATE = (0, 1, 2, 3), (7, 6, 4, 5)
GROUPS = ((0, 1, 2, 3), (4, 5), (6, 7))
NEAR = (1, 2, 7, 6)
NN = (((1,), (0,)), ((), ()))
NT = (((1,), (1,)), ((), ()))


def mm(a, b, dims=NN):
    return lax.dot_general(a, b, dims, preferred_element_type=F32)


def split2(v):
    hi = v.astype(BF16)
    return hi, (v - hi.astype(F32)).astype(BF16)


def split3(v):
    hi = v.astype(BF16)
    rest = v - hi.astype(F32)
    mid = rest.astype(BF16)
    return hi, mid, (rest - mid.astype(F32)).astype(BF16)


def exact(v, onehot, dims=NN):
    n = v.shape[0]
    r = mm(jnp.concatenate(split3(v), axis=0), onehot, dims)
    return (r[:n] + r[n : 2 * n]) + r[2 * n :]


def three(v, w, dims=NN):
    n = v.shape[0]
    vh, vl = split2(v)
    wh, wl = split2(w)
    r = mm(jnp.concatenate([vh, vl], axis=0), wh, dims)
    return (r[:n] + r[n:]) + mm(vh, wl, dims)


def kernel(
    res_hbm, agg_hbm, want_hbm, count_hbm, m_hbm, f_hbm, out_ref,
    res_ref, agg_ref, want_ref, count_ref, mbuf, fown, fmar, own, qout, ybuf, xg, nwant, hout, hin, ysum,
    i_sem, m_sem, f_sem, y_r, own_r, z_r, o_r, x_r, w_r, h_r, a_r, y_s, b_s, own_s, w_s, h_s, a_s, z_in, s_in,
):
    s = lax.axis_index("sub")
    b = lax.axis_index("blk")
    yl = s // (NZ * NX)
    z = lax.rem(s // NX, NZ)
    x = lax.rem(s, NX)
    mate = lax.rem(s + NZ * NX, NSUB)

    def zpos(d):
        return lax.rem(z + d, NZ)

    def at_z(d):
        return yl * (NZ * NX) + zpos(d) * NX + x

    def at_x(d):
        return s - x + lax.rem(x + d, NX)

    at_b = (b, b + 1 - 2 * lax.rem(b, 2), lax.rem(b + 2, NB), NB - 1 - b)
    nxt, prv = lax.rem(s + 1, NSUB), lax.rem(s + NSUB - 1, NSUB)

    inputs = [
        pltpu.make_async_copy(src, dst, i_sem.at[i])
        for i, (src, dst) in enumerate(
            [(res_hbm, res_ref), (agg_hbm, agg_ref), (want_hbm, want_ref), (count_hbm, count_ref)]
        )
    ]
    for c in inputs:
        c.start()

    def along_z(zp):
        return (yl * (NZ * NX) + zp * NX + x, b)

    cross_next, cross_prev = x == NX - 1, x == 0
    barrier = pltpu.get_barrier_semaphore()

    def signal(sem, to):
        pl.semaphore_signal(sem, inc=1, device_id=to, device_id_type=MESH)

    level = [(s, at_b[i]) for i in (2, 3, 1)] + [(mate, at_b[i]) for i in range(NB)] + [(at_x(d), b) for d in (2, 1, 3)]
    for p in level:
        signal(barrier, p)
    for zp in range(1, NZ):
        @pl.when(zp > z)
        def _():
            signal(barrier, along_z(zp))

    @pl.when(cross_next & (z < NZ - 1))
    def _():
        signal(barrier, (nxt, b))

    @pl.when(cross_prev & (z == 0))
    def _():
        signal(barrier, (prv, b))

    answers_prev, answers_next = cross_prev & (z > 0), cross_next & (z == NZ - 1)
    greeted = len(level) + z + jnp.where(answers_prev | answers_next, 1, 0)

    low_half = lax.broadcasted_iota(jnp.int32, (PR // 2, 128), 1) < 64

    def halves(even, odd):
        return jnp.where(low_half, even, pltpu.roll(odd, 64, 1)), jnp.where(low_half, pltpu.roll(even, 64, 1), odd)

    inputs[0].wait()
    inputs[1].wait()
    onehot = (lax.broadcasted_iota(jnp.int32, (CS, BL), 0) == agg_ref[...]).astype(BF16)
    part = exact(res_ref[...], onehot, NT)
    for h in range(2):
        wide = part[:, h * 128 : (h + 1) * 128]
        even, odd = halves(wide[: PR // 2], wide[PR // 2 :])
        qout[2 * h] = even
        qout[2 * h + 1] = odd

    pl.semaphore_wait(barrier, greeted)

    def remote(src, dst, ss, rs, to):
        return pltpu.make_async_remote_copy(
            src_ref=src, dst_ref=dst, send_sem=ss, recv_sem=rs, device_id=to, device_id_type=MESH
        )

    def send(*args):
        remote(*args).start()

    def arrived(ref, sem):
        remote(ref, ref, b_s, sem, (s, at_b[1])).wait_recv()

    def departed(ref, sem):
        remote(ref, ref, sem, y_r, (s, at_b[1])).wait_send()

    for other, i in ((0, 2), (0, 3), (1, 0), (1, 1), (1, 2), (1, 3), (0, 1)):
        to = at_b[i]
        send(qout.at[to], ybuf.at[i + NB * other - 1], y_s, y_r, (mate if other else s, to))
    for zp in range(NZ - 1):
        @pl.when(zp < z)
        def _():
            signal(z_in, along_z(zp))

    @pl.when(answers_prev)
    def _():
        signal(s_in, (prv, b))

    @pl.when(answers_next)
    def _():
        signal(s_in, (nxt, b))

    for i in range(NB):
        rows = pl.ds(pl.multiple_of(HM + at_b[i] * BL, 256), BL)
        pltpu.make_async_copy(f_hbm.at[0, rows, :], fown.at[i], f_sem.at[min(i, 1)]).start()
    for side in range(2):
        rows = pl.ds(side * (HM + NB * BL), HM)
        pltpu.make_async_copy(f_hbm.at[0, rows, :], fmar.at[side], f_sem.at[2]).start()
    for g, group in enumerate(GROUPS):
        for zp in group:
            for l in range(NY):
                cols = pl.ds(l * (NZ * CS) + zp * CS, CS)
                pltpu.make_async_copy(m_hbm.at[:, 0, cols], mbuf.at[zp, l], m_sem.at[g]).start()

    def loaded(ref, sem):
        pltpu.make_async_copy(ref, ref, sem).wait()

    loaded(fown.at[0], f_sem.at[0])
    fine = three(res_ref[...], fown[0])

    arrived(ybuf, y_r)
    mine = (qout[b] + ybuf[0]) + (ybuf[1] + ybuf[2])
    theirs = (ybuf[3] + ybuf[4]) + (ybuf[5] + ybuf[6])
    slot = z * NX + x
    xg[slot, pl.ds(pl.multiple_of(yl * 16, 16), 16), :] = mine
    xg[slot, pl.ds(pl.multiple_of((1 - yl) * 16, 16), 16), :] = theirs

    def group_of(zp):
        return jnp.where(zp >= 6, 2, jnp.where(zp >= 4, 1, 0)) if not isinstance(zp, int) else max(0, zp // 2 - 1)

    def block(zp, e):
        return xg.at[zp * NX + lax.rem(x + NX - e, NX)]

    def near(zp):
        d = lax.rem(z + NZ - zp, NZ)
        return (d == 1) | (d == 2) | (d == 6) | (d == 7)

    def z_copy(zp):
        return remote(block(z, 0), block(z, 0), b_s, z_r.at[z], along_z(zp))

    def v_copy(d):
        return remote(block(z, 2), block(z, 2), b_s, x_r.at[group_of(z)], (at_z(d), b))

    def x_copy(zp, e):
        return remote(block(zp, 0), block(zp, 0), b_s, x_r.at[group_of(zp)], (at_x(e), b))

    def forward(zp):
        @pl.when(zp != z)
        def _():
            arrived(block(zp, 0), z_r.at[zp])

            @pl.when(jnp.logical_not(near(zp)))
            def _():
                x_copy(zp, 2).start()

            x_copy(zp, 1).start()
            x_copy(zp, 3).start()

    for zp in range(NZ - 1):
        @pl.when(zp < z)
        def _():
            z_copy(zp).start()
    send(block(z, 0), block(z, 0), b_s, o_r, (at_x(2), b))
    for e in (1, 3):
        x_copy(z, e).start()
    for i in (2, 3, 1):
        send(res_ref, own.at[i - 1], own_s, own_r, (s, at_b[i]))

    @pl.when(z < NZ - 1)
    def _():
        pl.semaphore_wait(z_in, NZ - 1 - z)

    for zp in range(1, NZ):
        @pl.when(zp > z)
        def _():
            z_copy(zp).start()
    inputs[2].wait()

    @pl.when((cross_next & (z < NZ - 1)) | (cross_prev & (z == 0)))
    def _():
        pl.semaphore_wait(s_in, 1)

    send(want_ref, nwant.at[0], w_s, w_r.at[0], (nxt, b))
    send(want_ref, nwant.at[1], w_s, w_r.at[1], (prv, b))

    for zp in EARLY:
        forward(zp)
    arrived(block(z, 2), o_r)
    for d in NEAR:
        v_copy(d).start()

    def margin(side):
        arrived(nwant.at[side], w_r.at[side])
        wanted = nwant[side, 0, 1 - side : 2 - side, :]
        total = None
        for i in range(NB):
            rows = lax.broadcasted_iota(jnp.int32, (BL, HM), 0) + at_b[i] * BL
            r = exact(res_ref[...] if i == 0 else own[i - 1], (rows == wanted).astype(BF16))
            total = r if total is None else total + r
        hout[side] = total
        send(hout.at[side], hin.at[1 - side], h_s, h_r, (nxt if side else prv, b))

    late_prev = cross_prev & (z == 0)
    arrived(own, own_r)
    margin(1)

    @pl.when(jnp.logical_not(late_prev))
    def _():
        margin(0)

    def products(g):
        zps = GROUPS[g]
        first, n = zps[0] * NX, NX * len(zps) - len(zps)
        has_own = (z >= zps[0]) & (z <= zps[-1])

        @pl.when(has_own)
        def _():
            arrived(xg.at[pl.ds(first, n - 1)], x_r.at[g])

        @pl.when(jnp.logical_not(has_own))
        def _():
            arrived(xg.at[pl.ds(first, n)], x_r.at[g])

        loaded(mbuf.at[pl.ds(zps[0], len(zps))], m_sem.at[g])
        total = None
        for zp in zps:
            for l in range(NY):
                cols = []
                for h in range(2):
                    even = xg[zp * NX + 2 * h, 16 * l : 16 * l + 16, :]
                    odd = xg[zp * NX + 2 * h + 1, 16 * l : 16 * l + 16, :]
                    cols.append(jnp.concatenate(halves(even, odd), axis=0))
                r = three(jnp.concatenate(cols, axis=1), mbuf[zp, l], NT)
                total = r if total is None else total + r
        return total

    for zp in LATE:
        forward(zp)

    @pl.when(late_prev)
    def _():
        margin(0)

    coarse = products(0)
    coarse += products(2)
    coarse += products(1)
    ysum[0] = coarse
    for i in (2, 3, 1):
        send(ysum.at[0], ysum.at[i], a_s, a_r, (s, at_b[i]))

    loaded(fown.at[pl.ds(1, NB - 1)], f_sem.at[1])
    for i in range(1, NB):
        fine += three(own[i - 1], fown[i])
    inputs[3].wait()
    slots = lax.broadcasted_iota(jnp.int32, (PR, HM), 1)
    arrived(hin, h_r)
    loaded(fmar, f_sem.at[2])
    for side in range(2):
        edge = s == (0 if side == 0 else NSUB - 1)
        kept = jnp.where(edge, 0, count_ref[0, side])
        fine += three(jnp.where(slots < kept, hin[side], 0.0), fmar[side])

    arrived(ysum.at[pl.ds(1, NB - 1)], a_r)
    coarse = (ysum[0] + ysum[1]) + (ysum[2] + ysum[3])
    out_ref[...] = fine + exact(coarse, onehot)
    departed(ybuf, y_s)
    departed(xg.at[pl.ds(0, 31)], b_s)
    departed(own, own_s)
    departed(nwant, w_s)
    departed(hout, h_s)
    departed(ysum.at[pl.ds(1, NB - 1)], a_s)


def on_device(residual, fine_inverse, coarse_inverse, wanted_rows, wanted_count, aggregate):
    vmem = pl.BlockSpec(memory_space=pltpu.VMEM)
    hbm = pl.BlockSpec(memory_space=pl.ANY)
    dma = pltpu.SemaphoreType.DMA
    return pl.pallas_call(
        kernel,
        out_shape=jax.ShapeDtypeStruct((PR, BL), F32),
        in_specs=[hbm] * 6,
        out_specs=vmem,
        scratch_shapes=[
            pltpu.VMEM((PR, BL), F32),
            pltpu.VMEM((1, BL), jnp.int32),
            pltpu.VMEM((1, 2, HM), jnp.int32),
            pltpu.SMEM((1, 2), jnp.int32),
            pltpu.VMEM((NZ, NY, CS, CS), F32),
            pltpu.VMEM((NB, BL, BL), F32),
            pltpu.VMEM((2, HM, BL), F32),
            pltpu.VMEM((NB - 1, PR, BL), F32),
            pltpu.VMEM((NB, PR // 2, 128), F32),
            pltpu.VMEM((2 * NB - 1, PR // 2, 128), F32),
            pltpu.VMEM((NZ * NX, PR, 128), F32),
            pltpu.VMEM((2, 1, 2, HM), jnp.int32),
            pltpu.VMEM((2, PR, HM), F32),
            pltpu.VMEM((2, PR, HM), F32),
            pltpu.VMEM((NB, PR, CS), F32),
            dma((4,)), dma((3,)), dma((3,)),
            dma, dma, dma((NZ,)), dma, dma((3,)), dma((2,)), dma, dma,
            dma, dma, dma, dma, dma, dma,
            pltpu.SemaphoreType.REGULAR, pltpu.SemaphoreType.REGULAR,
        ],
        compiler_params=pltpu.CompilerParams(
            collective_id=0, has_side_effects=True, vmem_limit_bytes=48 * 1024 * 1024
        ),
        name="schwarz",
    )(*[pltpu.with_memory_space_constraint(v, pltpu.HBM) for v in (residual, aggregate.reshape(1, BL), wanted_rows, wanted_count, coarse_inverse, fine_inverse)])


def solution(mesh):
    in_specs = (
        P(None, ("sub", "blk")),
        P("sub", None, "blk"),
        P("sub", "blk", None),
        P("sub", None, None),
        P("sub", None),
        P(("sub", "blk")),
    )
    out_specs = P(None, ("sub", "blk"))
    return jax.shard_map(
        on_device, mesh=mesh, in_specs=in_specs, out_specs=out_specs, check_vma=False
    )
```

```python
import jax
import jax.numpy as jnp
from jax import lax
from jax.experimental import pallas as pl
from jax.experimental.pallas import tpu as pltpu
from jax.sharding import PartitionSpec as P

NX, NZ, NY = 4, 8, 2
NB = 4
NSUB = NX * NZ * NY
PR = 32
BL = 512
CS = 256
HM = 256
F32, BF16 = jnp.float32, jnp.bfloat16
MESH = pl.DeviceIdType.MESH
EARLY, LATE = (0, 1, 2, 3), (7, 6, 4, 5)
GROUPS = ((0, 1, 2, 3), (4, 5), (6, 7))
NN = (((1,), (0,)), ((), ()))
NT = (((1,), (1,)), ((), ()))


def mm(a, b, dims=NN):
    return lax.dot_general(a, b, dims, preferred_element_type=F32)


def split2(v):
    hi = v.astype(BF16)
    return hi, (v - hi.astype(F32)).astype(BF16)


def split3(v):
    hi = v.astype(BF16)
    rest = v - hi.astype(F32)
    mid = rest.astype(BF16)
    return hi, mid, (rest - mid.astype(F32)).astype(BF16)


def exact(v, onehot, dims=NN):
    n = v.shape[0]
    r = mm(jnp.concatenate(split3(v), axis=0), onehot, dims)
    return (r[:n] + r[n : 2 * n]) + r[2 * n :]


def three(v, w, dims=NN):
    n = v.shape[0]
    vh, vl = split2(v)
    wh, wl = split2(w)
    r = mm(jnp.concatenate([vh, vl], axis=0), wh, dims)
    return (r[:n] + r[n:]) + mm(vh, wl, dims)


def kernel(
    res_hbm, agg_hbm, want_hbm, count_hbm, m_hbm, f_hbm, out_ref,
    res_ref, agg_ref, want_ref, count_ref, mbuf, fown, fmar, own, qout, ybuf, xg, nwant, hout, hin, ysum,
    i_sem, m_sem, f_sem, y_r, own_r, z_r, x_r, w_r, h_r, a_r, y_s, b_s, own_s, w_s, h_s, a_s, z_in, s_in,
):
    s = lax.axis_index("sub")
    b = lax.axis_index("blk")
    yl = s // (NZ * NX)
    z = lax.rem(s // NX, NZ)
    x = lax.rem(s, NX)
    mate = lax.rem(s + NZ * NX, NSUB)

    def at_x(d):
        return s - x + lax.rem(x + d, NX)

    at_b = (b, b + 1 - 2 * lax.rem(b, 2), lax.rem(b + 2, NB), NB - 1 - b)
    nxt, prv = lax.rem(s + 1, NSUB), lax.rem(s + NSUB - 1, NSUB)

    inputs = [
        pltpu.make_async_copy(src, dst, i_sem.at[i])
        for i, (src, dst) in enumerate(
            [(res_hbm, res_ref), (agg_hbm, agg_ref), (want_hbm, want_ref), (count_hbm, count_ref)]
        )
    ]
    for c in inputs:
        c.start()

    def along_z(zp):
        return (yl * (NZ * NX) + zp * NX + x, b)

    cross_next, cross_prev = x == NX - 1, x == 0
    barrier = pltpu.get_barrier_semaphore()

    def signal(sem, to):
        pl.semaphore_signal(sem, inc=1, device_id=to, device_id_type=MESH)

    level = [(s, at_b[i]) for i in (2, 3, 1)] + [(mate, at_b[i]) for i in range(NB)] + [(at_x(d), b) for d in (2, 1, 3)]
    for p in level:
        signal(barrier, p)
    for zp in range(1, NZ):
        @pl.when(zp > z)
        def _():
            signal(barrier, along_z(zp))

    @pl.when(cross_next & (z < NZ - 1))
    def _():
        signal(barrier, (nxt, b))

    @pl.when(cross_prev & (z == 0))
    def _():
        signal(barrier, (prv, b))

    answers_prev, answers_next = cross_prev & (z > 0), cross_next & (z == NZ - 1)
    greeted = len(level) + z + jnp.where(answers_prev | answers_next, 1, 0)

    low_half = lax.broadcasted_iota(jnp.int32, (PR // 2, 128), 1) < 64

    def halves(even, odd):
        return jnp.where(low_half, even, pltpu.roll(odd, 64, 1)), jnp.where(low_half, pltpu.roll(even, 64, 1), odd)

    inputs[0].wait()
    inputs[1].wait()
    onehot = (lax.broadcasted_iota(jnp.int32, (CS, BL), 0) == agg_ref[...]).astype(BF16)
    part = exact(res_ref[...], onehot, NT)
    for h in range(2):
        wide = part[:, h * 128 : (h + 1) * 128]
        even, odd = halves(wide[: PR // 2], wide[PR // 2 :])
        qout[2 * h] = even
        qout[2 * h + 1] = odd

    pl.semaphore_wait(barrier, greeted)

    def remote(src, dst, ss, rs, to):
        return pltpu.make_async_remote_copy(
            src_ref=src, dst_ref=dst, send_sem=ss, recv_sem=rs, device_id=to, device_id_type=MESH
        )

    def send(*args):
        remote(*args).start()

    def arrived(ref, sem):
        remote(ref, ref, b_s, sem, (s, at_b[1])).wait_recv()

    def departed(ref, sem):
        remote(ref, ref, sem, y_r, (s, at_b[1])).wait_send()

    for other, i in ((0, 2), (0, 3), (1, 0), (1, 1), (1, 2), (1, 3), (0, 1)):
        to = at_b[i]
        send(qout.at[to], ybuf.at[i + NB * other - 1], y_s, y_r, (mate if other else s, to))
    for zp in range(NZ - 1):
        @pl.when(zp < z)
        def _():
            signal(z_in, along_z(zp))

    @pl.when(answers_prev)
    def _():
        signal(s_in, (prv, b))

    @pl.when(answers_next)
    def _():
        signal(s_in, (nxt, b))

    for i in range(NB):
        rows = pl.ds(pl.multiple_of(HM + at_b[i] * BL, 256), BL)
        pltpu.make_async_copy(f_hbm.at[0, rows, :], fown.at[i], f_sem.at[min(i, 1)]).start()
    for side in range(2):
        rows = pl.ds(side * (HM + NB * BL), HM)
        pltpu.make_async_copy(f_hbm.at[0, rows, :], fmar.at[side], f_sem.at[2]).start()
    for g, group in enumerate(GROUPS):
        for zp in group:
            for l in range(NY):
                cols = pl.ds(l * (NZ * CS) + zp * CS, CS)
                pltpu.make_async_copy(m_hbm.at[:, 0, cols], mbuf.at[zp, l], m_sem.at[g]).start()

    def loaded(ref, sem):
        pltpu.make_async_copy(ref, ref, sem).wait()

    loaded(fown.at[0], f_sem.at[0])
    fine = three(res_ref[...], fown[0])

    arrived(ybuf, y_r)
    mine = (qout[b] + ybuf[0]) + (ybuf[1] + ybuf[2])
    theirs = (ybuf[3] + ybuf[4]) + (ybuf[5] + ybuf[6])
    slot = z * NX + x
    xg[slot, pl.ds(pl.multiple_of(yl * 16, 16), 16), :] = mine
    xg[slot, pl.ds(pl.multiple_of((1 - yl) * 16, 16), 16), :] = theirs

    def group_of(zp):
        return jnp.where(zp >= 6, 2, jnp.where(zp >= 4, 1, 0)) if not isinstance(zp, int) else max(0, zp // 2 - 1)

    def block(zp, e):
        return xg.at[zp * NX + lax.rem(x + NX - e, NX)]

    def z_copy(zp):
        return remote(block(z, 0), block(z, 0), b_s, z_r.at[z], along_z(zp))

    def x_copy(zp, e):
        return remote(block(zp, 0), block(zp, 0), b_s, x_r.at[group_of(zp)], (at_x(e), b))

    def forward(zp):
        @pl.when(zp != z)
        def _():
            arrived(block(zp, 0), z_r.at[zp])

            for e in (2, 1, 3):
                x_copy(zp, e).start()

    for zp in range(NZ - 1):
        @pl.when(zp < z)
        def _():
            z_copy(zp).start()
    for e in (2, 1, 3):
        x_copy(z, e).start()
    for i in (2, 3, 1):
        send(res_ref, own.at[i - 1], own_s, own_r, (s, at_b[i]))

    @pl.when(z < NZ - 1)
    def _():
        pl.semaphore_wait(z_in, NZ - 1 - z)

    for zp in range(1, NZ):
        @pl.when(zp > z)
        def _():
            z_copy(zp).start()
    inputs[2].wait()

    @pl.when((cross_next & (z < NZ - 1)) | (cross_prev & (z == 0)))
    def _():
        pl.semaphore_wait(s_in, 1)

    send(want_ref, nwant.at[0], w_s, w_r.at[0], (nxt, b))
    send(want_ref, nwant.at[1], w_s, w_r.at[1], (prv, b))

    for zp in EARLY:
        forward(zp)

    def margin(side):
        arrived(nwant.at[side], w_r.at[side])
        wanted = nwant[side, 0, 1 - side : 2 - side, :]
        total = None
        for i in range(NB):
            rows = lax.broadcasted_iota(jnp.int32, (BL, HM), 0) + at_b[i] * BL
            r = exact(res_ref[...] if i == 0 else own[i - 1], (rows == wanted).astype(BF16))
            total = r if total is None else total + r
        hout[side] = total
        send(hout.at[side], hin.at[1 - side], h_s, h_r, (nxt if side else prv, b))

    late_prev = cross_prev & (z == 0)
    arrived(own, own_r)
    margin(1)

    @pl.when(jnp.logical_not(late_prev))
    def _():
        margin(0)

    def products(g):
        zps = GROUPS[g]
        arrived(xg.at[pl.ds(zps[0] * NX, (NX - 1) * len(zps))], x_r.at[g])
        loaded(mbuf.at[pl.ds(zps[0], len(zps))], m_sem.at[g])
        total = None
        for zp in zps:
            for l in range(NY):
                cols = []
                for h in range(2):
                    even = xg[zp * NX + 2 * h, 16 * l : 16 * l + 16, :]
                    odd = xg[zp * NX + 2 * h + 1, 16 * l : 16 * l + 16, :]
                    cols.append(jnp.concatenate(halves(even, odd), axis=0))
                r = three(jnp.concatenate(cols, axis=1), mbuf[zp, l], NT)
                total = r if total is None else total + r
        return total

    for zp in LATE:
        forward(zp)

    @pl.when(late_prev)
    def _():
        margin(0)

    coarse = products(0)
    coarse += products(2)
    coarse += products(1)
    ysum[0] = coarse
    for i in (2, 3, 1):
        send(ysum.at[0], ysum.at[i], a_s, a_r, (s, at_b[i]))

    loaded(fown.at[pl.ds(1, NB - 1)], f_sem.at[1])
    for i in range(1, NB):
        fine += three(own[i - 1], fown[i])
    inputs[3].wait()
    slots = lax.broadcasted_iota(jnp.int32, (PR, HM), 1)
    arrived(hin, h_r)
    loaded(fmar, f_sem.at[2])
    for side in range(2):
        edge = s == (0 if side == 0 else NSUB - 1)
        kept = jnp.where(edge, 0, count_ref[0, side])
        fine += three(jnp.where(slots < kept, hin[side], 0.0), fmar[side])

    arrived(ysum.at[pl.ds(1, NB - 1)], a_r)
    coarse = (ysum[0] + ysum[1]) + (ysum[2] + ysum[3])
    out_ref[...] = fine + exact(coarse, onehot)
    departed(ybuf, y_s)
    departed(xg.at[pl.ds(0, 31)], b_s)
    departed(own, own_s)
    departed(nwant, w_s)
    departed(hout, h_s)
    departed(ysum.at[pl.ds(1, NB - 1)], a_s)


def on_device(residual, fine_inverse, coarse_inverse, wanted_rows, wanted_count, aggregate):
    vmem = pl.BlockSpec(memory_space=pltpu.VMEM)
    hbm = pl.BlockSpec(memory_space=pl.ANY)
    dma = pltpu.SemaphoreType.DMA
    return pl.pallas_call(
        kernel,
        out_shape=jax.ShapeDtypeStruct((PR, BL), F32),
        in_specs=[hbm] * 6,
        out_specs=vmem,
        scratch_shapes=[
            pltpu.VMEM((PR, BL), F32),
            pltpu.VMEM((1, BL), jnp.int32),
            pltpu.VMEM((1, 2, HM), jnp.int32),
            pltpu.SMEM((1, 2), jnp.int32),
            pltpu.VMEM((NZ, NY, CS, CS), F32),
            pltpu.VMEM((NB, BL, BL), F32),
            pltpu.VMEM((2, HM, BL), F32),
            pltpu.VMEM((NB - 1, PR, BL), F32),
            pltpu.VMEM((NB, PR // 2, 128), F32),
            pltpu.VMEM((2 * NB - 1, PR // 2, 128), F32),
            pltpu.VMEM((NZ * NX, PR, 128), F32),
            pltpu.VMEM((2, 1, 2, HM), jnp.int32),
            pltpu.VMEM((2, PR, HM), F32),
            pltpu.VMEM((2, PR, HM), F32),
            pltpu.VMEM((NB, PR, CS), F32),
            dma((4,)), dma((3,)), dma((3,)),
            dma, dma, dma((NZ,)), dma((3,)), dma((2,)), dma, dma,
            dma, dma, dma, dma, dma, dma,
            pltpu.SemaphoreType.REGULAR, pltpu.SemaphoreType.REGULAR,
        ],
        compiler_params=pltpu.CompilerParams(
            collective_id=0, has_side_effects=True, vmem_limit_bytes=48 * 1024 * 1024
        ),
        name="schwarz",
    )(*[pltpu.with_memory_space_constraint(v, pltpu.HBM) for v in (residual, aggregate.reshape(1, BL), wanted_rows, wanted_count, coarse_inverse, fine_inverse)])


def solution(mesh):
    in_specs = (
        P(None, ("sub", "blk")),
        P("sub", None, "blk"),
        P("sub", "blk", None),
        P("sub", None, None),
        P("sub", None),
        P(("sub", "blk")),
    )
    out_specs = P(None, ("sub", "blk"))
    return jax.shard_map(
        on_device, mesh=mesh, in_specs=in_specs, out_specs=out_specs, check_vma=False
    )
```

```python
import jax
import jax.numpy as jnp
from jax import lax
from jax.experimental import pallas as pl
from jax.experimental.pallas import tpu as pltpu
from jax.sharding import PartitionSpec as P

NX, NZ, NY = 4, 8, 2
NB = 4
NSUB = NX * NZ * NY
PR = 32
BL = 512
CS = 256
HM = 256
F32, BF16 = jnp.float32, jnp.bfloat16
MESH = pl.DeviceIdType.MESH
EARLY, LATE = (0, 1, 2, 3), (7, 6, 4, 5)
GROUPS = ((0, 1, 2, 3), (4, 5), (6, 7))
NN = (((1,), (0,)), ((), ()))
NT = (((1,), (1,)), ((), ()))


def mm(a, b, dims=NN):
    return lax.dot_general(a, b, dims, preferred_element_type=F32)


def split2(v):
    hi = v.astype(BF16)
    return hi, (v - hi.astype(F32)).astype(BF16)


def split3(v):
    hi = v.astype(BF16)
    rest = v - hi.astype(F32)
    mid = rest.astype(BF16)
    return hi, mid, (rest - mid.astype(F32)).astype(BF16)


def exact(v, onehot, dims=NN):
    n = v.shape[0]
    r = mm(jnp.concatenate(split3(v), axis=0), onehot, dims)
    return (r[:n] + r[n : 2 * n]) + r[2 * n :]


def three(v, w, dims=NN):
    n = v.shape[0]
    vh, vl = split2(v)
    wh, wl = split2(w)
    r = mm(jnp.concatenate([vh, vl], axis=0), wh, dims)
    return (r[:n] + r[n:]) + mm(vh, wl, dims)


def kernel(
    res_hbm, agg_hbm, want_hbm, count_hbm, m_hbm, f_hbm, out_ref,
    res_ref, agg_ref, want_ref, count_ref, mbuf, fown, fmar, own, qout, ybuf, xg, nwant, hout, hin, ysum,
    i_sem, m_sem, f_sem, y_r, own_r, z_r, x_r, w_r, h_r, a_r, y_s, b_s, own_s, w_s, h_s, a_s, z_in, s_in,
):
    s = lax.axis_index("sub")
    b = lax.axis_index("blk")
    yl = s // (NZ * NX)
    z = lax.rem(s // NX, NZ)
    x = lax.rem(s, NX)
    mate = lax.rem(s + NZ * NX, NSUB)

    def at_x(d):
        return s - x + lax.rem(x + d, NX)

    at_b = (b, b + 1 - 2 * lax.rem(b, 2), lax.rem(b + 2, NB), NB - 1 - b)
    nxt, prv = lax.rem(s + 1, NSUB), lax.rem(s + NSUB - 1, NSUB)

    inputs = [
        pltpu.make_async_copy(src, dst, i_sem.at[i])
        for i, (src, dst) in enumerate(
            [(res_hbm, res_ref), (agg_hbm, agg_ref), (want_hbm, want_ref), (count_hbm, count_ref)]
        )
    ]
    for c in inputs:
        c.start()

    def along_z(zp):
        return (yl * (NZ * NX) + zp * NX + x, b)

    cross_next, cross_prev = x == NX - 1, x == 0
    barrier = pltpu.get_barrier_semaphore()

    def signal(sem, to):
        pl.semaphore_signal(sem, inc=1, device_id=to, device_id_type=MESH)

    level = [(s, at_b[i]) for i in (2, 3, 1)] + [(mate, at_b[i]) for i in range(NB)] + [(at_x(d), b) for d in (2, 1, 3)]
    for p in level:
        signal(barrier, p)
    for zp in range(1, NZ):
        @pl.when(zp > z)
        def _():
            signal(barrier, along_z(zp))

    @pl.when(cross_next & (z < NZ - 1))
    def _():
        signal(barrier, (nxt, b))

    @pl.when(cross_prev & (z == 0))
    def _():
        signal(barrier, (prv, b))

    answers_prev, answers_next = cross_prev & (z > 0), cross_next & (z == NZ - 1)
    greeted = len(level) + z + jnp.where(answers_prev | answers_next, 1, 0)

    low_half = lax.broadcasted_iota(jnp.int32, (PR // 2, 128), 1) < 64

    def halves(even, odd):
        return jnp.where(low_half, even, pltpu.roll(odd, 64, 1)), jnp.where(low_half, pltpu.roll(even, 64, 1), odd)

    inputs[0].wait()
    inputs[1].wait()
    onehot = (lax.broadcasted_iota(jnp.int32, (CS, BL), 0) == agg_ref[...]).astype(BF16)
    part = exact(res_ref[...], onehot, NT)
    for h in range(2):
        wide = part[:, h * 128 : (h + 1) * 128]
        even, odd = halves(wide[: PR // 2], wide[PR // 2 :])
        qout[2 * h] = even
        qout[2 * h + 1] = odd

    pl.semaphore_wait(barrier, greeted)

    def remote(src, dst, ss, rs, to):
        return pltpu.make_async_remote_copy(
            src_ref=src, dst_ref=dst, send_sem=ss, recv_sem=rs, device_id=to, device_id_type=MESH
        )

    def send(*args):
        remote(*args).start()

    def arrived(ref, sem):
        remote(ref, ref, b_s, sem, (s, at_b[1])).wait_recv()

    def departed(ref, sem):
        remote(ref, ref, sem, y_r, (s, at_b[1])).wait_send()

    for other, i in ((0, 2), (0, 3), (1, 0), (1, 1), (1, 2), (1, 3), (0, 1)):
        to = at_b[i]
        send(qout.at[to], ybuf.at[i + NB * other - 1], y_s, y_r, (mate if other else s, to))
    for zp in range(NZ - 1):
        @pl.when(zp < z)
        def _():
            signal(z_in, along_z(zp))

    @pl.when(answers_prev)
    def _():
        signal(s_in, (prv, b))

    @pl.when(answers_next)
    def _():
        signal(s_in, (nxt, b))

    for i in range(NB):
        rows = pl.ds(pl.multiple_of(HM + at_b[i] * BL, 256), BL)
        pltpu.make_async_copy(f_hbm.at[0, rows, :], fown.at[i], f_sem.at[min(i, 1)]).start()
    for side in range(2):
        rows = pl.ds(side * (HM + NB * BL), HM)
        pltpu.make_async_copy(f_hbm.at[0, rows, :], fmar.at[side], f_sem.at[2]).start()
    for g, group in enumerate(GROUPS):
        for zp in group:
            for l in range(NY):
                cols = pl.ds(l * (NZ * CS) + zp * CS, CS)
                pltpu.make_async_copy(m_hbm.at[:, 0, cols], mbuf.at[zp, l], m_sem.at[g]).start()

    def loaded(ref, sem):
        pltpu.make_async_copy(ref, ref, sem).wait()

    loaded(fown.at[0], f_sem.at[0])
    fine = three(res_ref[...], fown[0])

    arrived(ybuf, y_r)
    mine = (qout[b] + ybuf[0]) + (ybuf[1] + ybuf[2])
    theirs = (ybuf[3] + ybuf[4]) + (ybuf[5] + ybuf[6])
    slot = z * NX + x
    xg[slot, pl.ds(pl.multiple_of(yl * 16, 16), 16), :] = mine
    xg[slot, pl.ds(pl.multiple_of((1 - yl) * 16, 16), 16), :] = theirs

    def group_of(zp):
        return jnp.where(zp >= 6, 2, jnp.where(zp >= 4, 1, 0)) if not isinstance(zp, int) else max(0, zp // 2 - 1)

    def block(zp, e):
        return xg.at[zp * NX + lax.rem(x + NX - e, NX)]

    def z_copy(zp):
        return remote(block(z, 0), block(z, 0), b_s, z_r.at[z], along_z(zp))

    def x_copy(zp, e):
        return remote(block(zp, 0), block(zp, 0), b_s, x_r.at[group_of(zp)], (at_x(e), b))

    def forward(zp):
        @pl.when(zp != z)
        def _():
            arrived(block(zp, 0), z_r.at[zp])

            for e in (2, 1, 3):
                x_copy(zp, e).start()

    for zp in range(NZ - 1):
        @pl.when(zp < z)
        def _():
            z_copy(zp).start()
    for e in (2, 1, 3):
        x_copy(z, e).start()
    for i in (2, 3, 1):
        send(res_ref, own.at[i - 1], own_s, own_r, (s, at_b[i]))

    @pl.when(z < NZ - 1)
    def _():
        pl.semaphore_wait(z_in, NZ - 1 - z)

    for zp in range(1, NZ):
        @pl.when(zp > z)
        def _():
            z_copy(zp).start()
    inputs[2].wait()

    @pl.when((cross_next & (z < NZ - 1)) | (cross_prev & (z == 0)))
    def _():
        pl.semaphore_wait(s_in, 1)

    send(want_ref, nwant.at[0], w_s, w_r.at[0], (nxt, b))
    send(want_ref, nwant.at[1], w_s, w_r.at[1], (prv, b))

    for zp in EARLY:
        forward(zp)

    def margin(side):
        arrived(nwant.at[side], w_r.at[side])
        wanted = nwant[side, 0, 1 - side : 2 - side, :]
        total = None
        for i in range(NB):
            rows = lax.broadcasted_iota(jnp.int32, (BL, HM), 0) + at_b[i] * BL
            r = exact(res_ref[...] if i == 0 else own[i - 1], (rows == wanted).astype(BF16))
            total = r if total is None else total + r
        hout[side] = total
        send(hout.at[side], hin.at[1 - side], h_s, h_r, (nxt if side else prv, b))

    def products(g):
        zps = GROUPS[g]
        arrived(xg.at[pl.ds(zps[0] * NX, (NX - 1) * len(zps))], x_r.at[g])
        loaded(mbuf.at[pl.ds(zps[0], len(zps))], m_sem.at[g])
        total = None
        for zp in zps:
            for l in range(NY):
                cols = []
                for h in range(2):
                    even = xg[zp * NX + 2 * h, 16 * l : 16 * l + 16, :]
                    odd = xg[zp * NX + 2 * h + 1, 16 * l : 16 * l + 16, :]
                    cols.append(jnp.concatenate(halves(even, odd), axis=0))
                r = three(jnp.concatenate(cols, axis=1), mbuf[zp, l], NT)
                total = r if total is None else total + r
        return total

    for zp in LATE:
        forward(zp)

    arrived(own, own_r)
    margin(1)
    margin(0)
    coarse = products(0)
    coarse += products(2)
    coarse += products(1)
    ysum[0] = coarse
    for i in (2, 3, 1):
        send(ysum.at[0], ysum.at[i], a_s, a_r, (s, at_b[i]))

    loaded(fown.at[pl.ds(1, NB - 1)], f_sem.at[1])
    for i in range(1, NB):
        fine += three(own[i - 1], fown[i])
    inputs[3].wait()
    slots = lax.broadcasted_iota(jnp.int32, (PR, HM), 1)
    arrived(hin, h_r)
    loaded(fmar, f_sem.at[2])
    for side in range(2):
        edge = s == (0 if side == 0 else NSUB - 1)
        kept = jnp.where(edge, 0, count_ref[0, side])
        fine += three(jnp.where(slots < kept, hin[side], 0.0), fmar[side])

    arrived(ysum.at[pl.ds(1, NB - 1)], a_r)
    coarse = (ysum[0] + ysum[1]) + (ysum[2] + ysum[3])
    out_ref[...] = fine + exact(coarse, onehot)
    departed(ybuf, y_s)
    departed(xg.at[pl.ds(0, 31)], b_s)
    departed(own, own_s)
    departed(nwant, w_s)
    departed(hout, h_s)
    departed(ysum.at[pl.ds(1, NB - 1)], a_s)


def on_device(residual, fine_inverse, coarse_inverse, wanted_rows, wanted_count, aggregate):
    vmem = pl.BlockSpec(memory_space=pltpu.VMEM)
    hbm = pl.BlockSpec(memory_space=pl.ANY)
    dma = pltpu.SemaphoreType.DMA
    return pl.pallas_call(
        kernel,
        out_shape=jax.ShapeDtypeStruct((PR, BL), F32),
        in_specs=[hbm] * 6,
        out_specs=vmem,
        scratch_shapes=[
            pltpu.VMEM((PR, BL), F32),
            pltpu.VMEM((1, BL), jnp.int32),
            pltpu.VMEM((1, 2, HM), jnp.int32),
            pltpu.SMEM((1, 2), jnp.int32),
            pltpu.VMEM((NZ, NY, CS, CS), F32),
            pltpu.VMEM((NB, BL, BL), F32),
            pltpu.VMEM((2, HM, BL), F32),
            pltpu.VMEM((NB - 1, PR, BL), F32),
            pltpu.VMEM((NB, PR // 2, 128), F32),
            pltpu.VMEM((2 * NB - 1, PR // 2, 128), F32),
            pltpu.VMEM((NZ * NX, PR, 128), F32),
            pltpu.VMEM((2, 1, 2, HM), jnp.int32),
            pltpu.VMEM((2, PR, HM), F32),
            pltpu.VMEM((2, PR, HM), F32),
            pltpu.VMEM((NB, PR, CS), F32),
            dma((4,)), dma((3,)), dma((3,)),
            dma, dma, dma((NZ,)), dma((3,)), dma((2,)), dma, dma,
            dma, dma, dma, dma, dma, dma,
            pltpu.SemaphoreType.REGULAR, pltpu.SemaphoreType.REGULAR,
        ],
        compiler_params=pltpu.CompilerParams(
            collective_id=0, has_side_effects=True, vmem_limit_bytes=48 * 1024 * 1024
        ),
        name="schwarz",
    )(*[pltpu.with_memory_space_constraint(v, pltpu.HBM) for v in (residual, aggregate.reshape(1, BL), wanted_rows, wanted_count, coarse_inverse, fine_inverse)])


def solution(mesh):
    in_specs = (
        P(None, ("sub", "blk")),
        P("sub", None, "blk"),
        P("sub", "blk", None),
        P("sub", None, None),
        P("sub", None),
        P(("sub", "blk")),
    )
    out_specs = P(None, ("sub", "blk"))
    return jax.shard_map(
        on_device, mesh=mesh, in_specs=in_specs, out_specs=out_specs, check_vma=False
    )
```
